512 devices in a mesh: seq: 64 (over y, z), head: 8 (over x, core).
Axes of the slice: x: 4, y: 8, z: 8, core: 2. Of those that a mesh axis runs over, the one named last changes fastest.
Arguments:
- queries: bfloat16 [16384, 2048], P('seq', 'head'), may hold values from -4 to 4
- first_pair_keys: bfloat16 [16384, 1024], P('seq', 'head'), may hold values from -4 to 4
- first_pair_values: bfloat16 [16384, 1024], P('seq', 'head'), may hold values from -6 to 6
- second_pair_keys: bfloat16 [16384, 1024], P('seq', 'head'), may hold values from -4 to 4
- second_pair_values: bfloat16 [16384, 1024], P('seq', 'head'), may hold values from -6 to 6
- out_weight: bfloat16 [2048, 8192], P('seq', 'head'), may hold values from -0.125 to 0.125
Outputs:
- attended: bfloat16 [16384, 2048], P('seq', 'head')
- projected: bfloat16 [16384, 8192], P('seq', 'head')
The draws below stay inside these ranges and needn't reach their ends.
All inputs are finite; a program needn't handle non-finite values.
Results may differ from the reference program's by a relative error of at most 0.0064.
Values may be sent and summed in bfloat16 or wider, within the bound.
No kernel may reach another device: no remote copies, remote signals or barrier semaphores. Data moves between devices by JAX's collectives and lax.ppermute only.
A program may use at most 64 MiB of HBM per device.

```python
import math
import jax
import jax.numpy as jnp
from jax import lax

HEAD_SIZE = 128
KEY_VALUE_HEADS = 8
GROUP_QUERIES = 2
HQ = 16
DM = 8192
FIRST_WINDOW = 512
SECOND_WINDOW = 32
SEQUENCE_TOKENS = 16384


def backdrop_fill(key, salt, shape):
    subkey = jax.random.fold_in(key, salt)
    return jnp.clip(jax.random.normal(subkey, shape, jnp.float32), -4.0, 4.0)


def draw_queries(key, part):
    value_entries = backdrop_fill(key, 11, (SEQUENCE_TOKENS, KEY_VALUE_HEADS, GROUP_QUERIES, HEAD_SIZE))
    return value_entries.reshape(SEQUENCE_TOKENS, KEY_VALUE_HEADS * GROUP_QUERIES * HEAD_SIZE).astype(jnp.bfloat16)


def draw_first_pair_keys(key, part):
    value_entries = backdrop_fill(key, 12, (SEQUENCE_TOKENS, KEY_VALUE_HEADS, HEAD_SIZE))
    return value_entries.reshape(SEQUENCE_TOKENS, KEY_VALUE_HEADS * HEAD_SIZE).astype(jnp.bfloat16)


def draw_second_pair_keys(key, part):
    value_entries = backdrop_fill(key, 13, (SEQUENCE_TOKENS, KEY_VALUE_HEADS, HEAD_SIZE))
    return value_entries.reshape(SEQUENCE_TOKENS, KEY_VALUE_HEADS * HEAD_SIZE).astype(jnp.bfloat16)


def block_levels(key, shape, shards, least, largest):
    factor_of, own = 1.0, jax.random.fold_in(key, 6)
    for axis_at, shards_of in shards:
        draws = jnp.exp(jax.random.uniform(jax.random.fold_in(own, axis_at), (shards_of,), jnp.float32, least / len(shards), largest / len(shards)))
        factor_of = factor_of * jnp.repeat(draws, shape[axis_at] // shards_of).reshape([-1 if axis == axis_at else 1 for axis in range(len(shape))])
    return factor_of


def noise(rng, dims, scale, limit, shards=(), kind=jnp.bfloat16):
    entries = jax.random.normal(rng, dims, jnp.float32) * scale
    if len(shards) > 0:
        entries = block_levels(rng, dims, shards, -0.22, 0.18) * entries
    return jnp.clip(entries, min=-limit, max=limit).astype(kind)


def setup_inputs(seed: int = 0) -> dict:
    keys = jax.random.split(jax.random.key(seed), 7)
    return {
        "queries": draw_queries(jax.random.fold_in(keys[6], 71), 0),
        "first_pair_keys": draw_first_pair_keys(jax.random.fold_in(keys[6], 71), 0),
        "first_pair_values": noise(keys[2], (SEQUENCE_TOKENS, KEY_VALUE_HEADS * HEAD_SIZE), 1.0, 6.0, ((0, 64), (1, 8))),
        "second_pair_keys": draw_second_pair_keys(jax.random.fold_in(keys[6], 71), 0),
        "second_pair_values": noise(keys[4], (SEQUENCE_TOKENS, KEY_VALUE_HEADS * HEAD_SIZE), 1.0, 6.0, ((0, 64), (1, 8))),
        "out_weight": noise(keys[5], (HQ * HEAD_SIZE, DM), (HQ * HEAD_SIZE) ** -0.5, 0.125, ((0, 64), (1, 8))),
    }


def attend_block(query_rows, first_rows, first_vals, second_win, second_vwin, query_pos, key_pos):
    score_scale = HEAD_SIZE ** -0.5
    query_mod = (query_rows.astype(jnp.float32)[:, None] * second_win.astype(jnp.float32)[:, :, :, None, :]).astype(jnp.bfloat16)
    scores = jnp.einsum("itvgd,jvd->ivgtj", query_mod.astype(jnp.float32), first_rows.astype(jnp.float32)) * score_scale
    key_lag = query_pos[:, None] - key_pos[None, :]
    first_ok = (key_lag >= 0) & (key_lag < FIRST_WINDOW) & (key_pos[None, :] >= 0)
    offsets = jnp.arange(SECOND_WINDOW, dtype=jnp.int32)
    second_ok = (query_pos[:, None] - offsets[None, :]) >= 0
    is_valid = first_ok[:, None, None, None, :] & second_ok[:, None, None, :, None]
    scores = jnp.where(is_valid, scores, -jnp.inf)
    row_top = jnp.max(scores, axis=(3, 4), keepdims=True)
    row_weights = jnp.exp(scores - row_top)
    row_sum = jnp.sum(row_weights, axis=(3, 4))
    weights_bf = row_weights.astype(jnp.bfloat16)
    first_mix = jnp.einsum("ivgtj,jvd->ivgtd", weights_bf.astype(jnp.float32), first_vals.astype(jnp.float32))
    second_side = jnp.transpose(second_vwin, (0, 2, 1, 3)).astype(jnp.float32)[:, :, None]
    combined = jnp.sum(first_mix * second_side, axis=3)
    return (combined / row_sum[..., None]).astype(jnp.bfloat16)


def reference(queries, first_pair_keys, first_pair_values, second_pair_keys, second_pair_values, out_weight):
    token_count = queries.shape[0]
    block_rows = math.gcd(128, token_count)
    query_head_count = queries.reshape(token_count, KEY_VALUE_HEADS, GROUP_QUERIES, HEAD_SIZE)
    leading_first = jnp.zeros((FIRST_WINDOW, KEY_VALUE_HEADS, HEAD_SIZE), jnp.bfloat16)
    leading_second = jnp.zeros((SECOND_WINDOW - 1, KEY_VALUE_HEADS, HEAD_SIZE), jnp.bfloat16)
    padded_first_keys = jnp.concatenate([leading_first, first_pair_keys.reshape(token_count, KEY_VALUE_HEADS, HEAD_SIZE)], axis=0)
    padded_first_values = jnp.concatenate([leading_first, first_pair_values.reshape(token_count, KEY_VALUE_HEADS, HEAD_SIZE)], axis=0)
    padded_second_keys = jnp.concatenate([leading_second, second_pair_keys.reshape(token_count, KEY_VALUE_HEADS, HEAD_SIZE)], axis=0)
    padded_second_values = jnp.concatenate([leading_second, second_pair_values.reshape(token_count, KEY_VALUE_HEADS, HEAD_SIZE)], axis=0)

    def one_block(block_index):
        block_start = (block_index * block_rows).astype(jnp.int32)
        query_rows = lax.dynamic_slice_in_dim(query_head_count, block_start, block_rows, 0)
        first_rows = lax.dynamic_slice_in_dim(padded_first_keys, block_start, block_rows + FIRST_WINDOW, 0)
        first_vals = lax.dynamic_slice_in_dim(padded_first_values, block_start, block_rows + FIRST_WINDOW, 0)
        near_keys = lax.dynamic_slice_in_dim(padded_second_keys, block_start, block_rows + SECOND_WINDOW - 1, 0)
        near_vals = lax.dynamic_slice_in_dim(padded_second_values, block_start, block_rows + SECOND_WINDOW - 1, 0)
        second_win = jnp.stack([near_keys[SECOND_WINDOW - 1 - lag_step: SECOND_WINDOW - 1 - lag_step + block_rows] for lag_step in range(SECOND_WINDOW)], axis=1)
        second_vwin = jnp.stack([near_vals[SECOND_WINDOW - 1 - lag_step: SECOND_WINDOW - 1 - lag_step + block_rows] for lag_step in range(SECOND_WINDOW)], axis=1)
        query_pos = block_start + jnp.arange(block_rows, dtype=jnp.int32)
        key_pos = block_start - FIRST_WINDOW + jnp.arange(block_rows + FIRST_WINDOW, dtype=jnp.int32)
        return attend_block(query_rows, first_rows, first_vals, second_win, second_vwin, query_pos, key_pos)

    block_list = lax.map(one_block, jnp.arange(token_count // block_rows, dtype=jnp.int32))
    attended = block_list.reshape(token_count, KEY_VALUE_HEADS * GROUP_QUERIES * HEAD_SIZE)
    projected = jnp.dot(attended, out_weight, preferred_element_type=jnp.float32).astype(jnp.bfloat16)
    return attended, projected
```

```python
import functools
import math

import jax
import jax.numpy as jnp
from jax import lax
from jax.experimental import pallas as pl
from jax.experimental.pallas import tpu as pltpu
from jax.sharding import PartitionSpec as P

HEAD = 128
GROUP = 2
FIRST = 512
SECOND = 32
ROWS = 256
BLOCK = 128
KEYS = FIRST + BLOCK
STEP = 8
SCALE = HEAD ** (-0.5) * math.log2(math.e)


def attend(b, g, index, queries, far, near, keys, values, second_keys, second_values, out, k_all, v_all, k2, v2, kept, score, total, top):
    first_block = index[0]
    base = b * BLOCK
    spare = jnp.broadcast_to(keys[0:1, :].astype(jnp.float32), (BLOCK, HEAD)).astype(jnp.bfloat16)
    zero = jnp.zeros((BLOCK, HEAD), jnp.bfloat16)
    one = jnp.ones((BLOCK, HEAD), jnp.bfloat16)

    for piece in range(KEYS // BLOCK):
        slot, at = divmod(base + piece * BLOCK, ROWS)
        to = slice(piece * BLOCK, (piece + 1) * BLOCK)
        if slot == 2:
            k_all[to, :] = keys[at : at + BLOCK, :]
            v_all[to, :HEAD] = values[at : at + BLOCK, :]
            v_all[to, HEAD:] = one
        else:
            source = (far, near)[slot]
            held = first_block >= 2 - slot
            k_all[to, :] = jnp.where(held, source[at : at + BLOCK, :], spare)
            v_all[to, :HEAD] = jnp.where(held, source[ROWS + at : ROWS + at + BLOCK, :], zero)
            v_all[to, HEAD:] = jnp.where(held, one, zero)

    if b == 0:
        held = first_block >= 1
        edge_k = near[2 * ROWS : 2 * ROWS + SECOND, :].astype(jnp.float32)
        edge_v = near[2 * ROWS + SECOND : 2 * ROWS + 2 * SECOND, :].astype(jnp.float32)
        spare2 = jnp.broadcast_to(second_keys[0:1, :].astype(jnp.float32), (SECOND, HEAD))
        kept[0, 0:SECOND, :] = jnp.where(held, edge_k, spare2)
        kept[1, 0:SECOND, :] = jnp.where(held, edge_v, jnp.zeros_like(edge_v))
        kept[2, 0:SECOND, :] = jnp.where(held, jnp.ones_like(edge_v), jnp.zeros_like(edge_v))
        kept[0, SECOND:, :] = second_keys[:BLOCK, :].astype(jnp.float32)
        kept[1, SECOND:, :] = second_values[:BLOCK, :].astype(jnp.float32)
        kept[2, SECOND:, :] = jnp.ones((BLOCK, HEAD), jnp.float32)
    else:
        kept[0] = second_keys[base - SECOND : base + BLOCK, :].astype(jnp.float32)
        kept[1] = second_values[base - SECOND : base + BLOCK, :].astype(jnp.float32)
    for r in range(STEP):
        k2[r, STEP:, :] = kept[0, STEP - r : SECOND + BLOCK - r, :]
        v2[r, STEP:, :HEAD] = kept[1, STEP - r : SECOND + BLOCK - r, :]
        if b == 0:
            v2[r, STEP:, HEAD:] = kept[2, STEP - r : SECOND + BLOCK - r, :]
        else:
            v2[r, STEP:, HEAD:] = jnp.ones((SECOND + BLOCK - STEP, HEAD), jnp.float32)

    row = lax.broadcasted_iota(jnp.int32, (BLOCK, HEAD), 0)
    col = lax.broadcasted_iota(jnp.int32, (BLOCK, HEAD), 1)
    upper = col > row
    q = queries[base : base + BLOCK, g * HEAD : (g + 1) * HEAD].astype(jnp.float32)
    k_win = k_all[...]
    v_win = v_all[...]
    top[...] = jnp.full((BLOCK, HEAD), -1e30, jnp.float32)
    total[...] = jnp.zeros((BLOCK, 2 * HEAD), jnp.float32)

    def step(a, _):
        start = pl.multiple_of(SECOND - STEP * a, STEP)
        most = None
        for r in range(STEP):
            mod = (q * k2[r, pl.ds(start, BLOCK), :]).astype(jnp.bfloat16)
            s = lax.dot_general(mod, k_win, (((1,), (1,)), ((), ())), preferred_element_type=jnp.float32)
            edge = jnp.where(upper, s[:, :HEAD], s[:, FIRST:])
            score[r, :, :HEAD] = edge
            score[r, :, HEAD:] = s[:, HEAD:FIRST]
            here = jnp.maximum(
                jnp.maximum(edge, s[:, HEAD : 2 * HEAD]),
                jnp.maximum(s[:, 2 * HEAD : 3 * HEAD], s[:, 3 * HEAD : FIRST]),
            )
            most = here if most is None else jnp.maximum(most, here)
        old = top[...]
        new = jnp.maximum(old, jnp.max(most, axis=1, keepdims=True))
        top[...] = new
        shift = new * SCALE
        shrink = jnp.exp2(old * SCALE - shift)
        acc = total[...] * jnp.concatenate([shrink, shrink], axis=1)
        for r in range(STEP):
            parts = [
                jnp.exp2(score[r, :, k * HEAD : (k + 1) * HEAD] * SCALE - shift) for k in range(FIRST // HEAD)
            ]
            nothing = jnp.zeros_like(parts[0])
            ends = [jnp.where(upper, parts[0], nothing), jnp.where(upper, nothing, parts[0])]
            weights = jnp.concatenate(ends[:1] + parts[1:] + ends[1:], axis=1).astype(jnp.bfloat16)
            mix = jnp.dot(weights, v_win, preferred_element_type=jnp.float32)
            acc = acc + mix * v2[r, pl.ds(start, BLOCK), :]
        total[...] = acc
        return 0

    lax.fori_loop(0, SECOND // STEP, step, 0)
    out[...] = (total[:, :HEAD] / total[:, HEAD:]).astype(jnp.bfloat16)


def attention(b, g, *operands):
    vmem = pl.BlockSpec(memory_space=pltpu.VMEM)
    return pl.pallas_call(
        functools.partial(attend, b, g),
        out_shape=jax.ShapeDtypeStruct((BLOCK, HEAD), jnp.bfloat16),
        in_specs=[pl.BlockSpec(memory_space=pltpu.SMEM)] + [vmem] * 7,
        out_specs=vmem,
        scratch_shapes=[
            pltpu.VMEM((KEYS, HEAD), jnp.bfloat16),
            pltpu.VMEM((KEYS, 2 * HEAD), jnp.bfloat16),
            pltpu.VMEM((STEP, BLOCK + SECOND, HEAD), jnp.float32),
            pltpu.VMEM((STEP, BLOCK + SECOND, 2 * HEAD), jnp.float32),
            pltpu.VMEM((3, BLOCK + SECOND, HEAD), jnp.float32),
            pltpu.VMEM((STEP, BLOCK, FIRST), jnp.float32),
            pltpu.VMEM((BLOCK, 2 * HEAD), jnp.float32),
            pltpu.VMEM((BLOCK, HEAD), jnp.float32),
        ],
        compiler_params=pltpu.CompilerParams(vmem_limit_bytes=24 * 1024 * 1024),
        cost_estimate=pl.CostEstimate(flops=3_000_000_000, bytes_accessed=1_000_000, transcendentals=3_000_000),
        name="attend",
    )(*operands)


def project(order, direct, swapped, weight, out, total):
    for k in range(SIDE):
        at = order[k]
        rows = jnp.where(order[SIDE + k] == 0, direct[at], swapped[at])
        piece = jnp.dot(rows, weight[k], preferred_element_type=jnp.float32)
        if k == 0:
            total[...] = piece
        elif k < SIDE - 1:
            total[...] += piece
        else:
            out[...] = (total[...] + piece).astype(jnp.bfloat16)


def projection(order, direct, swapped, weight):
    width = weight.shape[-1]
    vmem = pl.BlockSpec(memory_space=pltpu.VMEM)
    return pl.pallas_call(
        project,
        out_shape=jax.ShapeDtypeStruct((ROWS, width), jnp.bfloat16),
        in_specs=[pl.BlockSpec(memory_space=pltpu.SMEM)] + [vmem] * 3,
        out_specs=vmem,
        scratch_shapes=[pltpu.VMEM((ROWS, width), jnp.float32)],
        compiler_params=pltpu.CompilerParams(vmem_limit_bytes=24 * 1024 * 1024),
        cost_estimate=pl.CostEstimate(flops=1_100_000_000, bytes_accessed=6_000_000, transcendentals=0),
        name="project",
    )(order, direct, swapped, weight)


SIDE = 8
CHIPS = 4
HOPS = (0, 1, 3, 2)


def shifted(x, by):
    size = lax.axis_size("seq")
    return lax.ppermute(x, "seq", [(i, i + by) for i in range(size - by)])


def on_device(queries, first_keys, first_values, second_keys, second_values, out_weight):
    width = out_weight.shape[1]
    packed = jnp.concatenate([first_keys, first_values, second_keys[-SECOND:], second_values[-SECOND:]], axis=0)
    near = shifted(packed, 1)
    far = shifted(packed, 2)
    weight = lax.all_gather(out_weight, "seq", axis=0, tiled=True).reshape(SIDE, ROWS, width)
    seq = lax.axis_index("seq").astype(jnp.int32)
    head = lax.axis_index("head").astype(jnp.int32)
    operands = (seq.reshape(1), queries, far, near, first_keys, first_values, second_keys, second_values)
    pieces = [attention(b, g, *operands) for b in range(ROWS // BLOCK) for g in range(GROUP)]
    attended = jnp.concatenate(
        [jnp.concatenate(pieces[:2], axis=1), jnp.concatenate(pieces[2:], axis=1)], axis=0
    )
    direct = [attended]
    for hop in HOPS[1:]:
        pairs = [(2 * x + c, 2 * ((x + hop) % CHIPS) + c) for x in range(CHIPS) for c in range(2)]
        direct.append(lax.ppermute(attended, "head", pairs))
    direct = jnp.stack(direct)
    swapped = lax.ppermute(direct, "head", [(2 * x + c, 2 * x + 1 - c) for x in range(CHIPS) for c in range(2)])
    chip, core = lax.div(head, 2), lax.rem(head, 2)
    owner = jnp.arange(SIDE, dtype=jnp.int32)
    distance = lax.rem(chip - lax.div(owner, 2) + CHIPS, CHIPS)
    place = jnp.where(distance < 2, distance, 5 - distance)
    part = jnp.where(lax.rem(owner, 2) == core, 0, 1)
    order = jnp.concatenate([place, part]).astype(jnp.int32)
    return attended, projection(order, direct, swapped, weight)


def solution(mesh):
    spec = P("seq", "head")
    return jax.shard_map(on_device, mesh=mesh, in_specs=(spec,) * 6, out_specs=(spec, spec), check_vma=False)
```

```python
import math

import jax
import jax.numpy as jnp
from jax import lax
from jax.experimental import pallas as pl
from jax.experimental.pallas import tpu as pltpu
from jax.sharding import PartitionSpec as P


HEAD = 128
GROUP = 2
FIRST = 512
SECOND = 32
ROWS = 256
BLOCK = 128
KEYS = FIRST + BLOCK
STEP = 8
SCALE = HEAD ** (-0.5) * math.log2(math.e)


def attend(index, *refs):
    sources, out, held_refs, sems = refs[:7], refs[7], refs[8:15], refs[15]
    k_all, v_all, k2, v2, kept, score, total, top = refs[16:]
    moves = [pltpu.make_async_copy(src, dst, sems.at[i]) for i, (src, dst) in enumerate(zip(sources, held_refs))]
    for move in moves:
        move.start()
    for move in moves:
        move.wait()
    queries, far, near, keys, values, second_keys, second_values = held_refs
    first_block = index[0]
    spare = jnp.broadcast_to(keys[0:1, :].astype(jnp.float32), (ROWS, HEAD)).astype(jnp.bfloat16)
    zero = jnp.zeros((ROWS, HEAD), jnp.bfloat16)
    one = jnp.ones((ROWS, HEAD), jnp.bfloat16)
    row = lax.broadcasted_iota(jnp.int32, (BLOCK, HEAD), 0)
    col = lax.broadcasted_iota(jnp.int32, (BLOCK, HEAD), 1)
    upper = col > row

    for slot, source in enumerate((far, near)):
        held = first_block >= 2 - slot
        to = slice(slot * ROWS, (slot + 1) * ROWS)
        k_all[to, :] = jnp.where(held, source[:ROWS, :], spare)
        v_all[to, :HEAD] = jnp.where(held, source[ROWS : 2 * ROWS, :], zero)
        v_all[to, HEAD:] = jnp.where(held, one, zero)
    k_all[2 * ROWS :, :] = keys[...]
    v_all[2 * ROWS :, :HEAD] = values[...]
    v_all[2 * ROWS :, HEAD:] = one

    for b in range(ROWS // BLOCK):
        base = b * BLOCK
        if b == 0:
            held = first_block >= 1
            edge_k = near[2 * ROWS : 2 * ROWS + SECOND, :].astype(jnp.float32)
            edge_v = near[2 * ROWS + SECOND : 2 * ROWS + 2 * SECOND, :].astype(jnp.float32)
            spare2 = jnp.broadcast_to(second_keys[0:1, :].astype(jnp.float32), (SECOND, HEAD))
            kept[0, 0:SECOND, :] = jnp.where(held, edge_k, spare2)
            kept[1, 0:SECOND, :] = jnp.where(held, edge_v, jnp.zeros_like(edge_v))
            kept[2, 0:SECOND, :] = jnp.where(held, jnp.ones_like(edge_v), jnp.zeros_like(edge_v))
            kept[0, SECOND:, :] = second_keys[:BLOCK, :].astype(jnp.float32)
            kept[1, SECOND:, :] = second_values[:BLOCK, :].astype(jnp.float32)
            kept[2, SECOND:, :] = jnp.ones((BLOCK, HEAD), jnp.float32)
        else:
            kept[0] = second_keys[base - SECOND : base + BLOCK, :].astype(jnp.float32)
            kept[1] = second_values[base - SECOND : base + BLOCK, :].astype(jnp.float32)
        for r in range(STEP):
            k2[r, STEP:, :] = kept[0, STEP - r : SECOND + BLOCK - r, :]
            v2[r, STEP:, :HEAD] = kept[1, STEP - r : SECOND + BLOCK - r, :]
            if b == 0:
                v2[r, STEP:, HEAD:] = kept[2, STEP - r : SECOND + BLOCK - r, :]
            else:
                v2[r, STEP:, HEAD:] = jnp.ones((SECOND + BLOCK - STEP, HEAD), jnp.float32)

        k_win = k_all[base : base + KEYS, :]
        v_win = v_all[base : base + KEYS, :]
        for g in range(GROUP):
            q = queries[base : base + BLOCK, g * HEAD : (g + 1) * HEAD].astype(jnp.float32)

            def scored(a, r, q=q, k_win=k_win):
                start = SECOND - STEP * a
                mod = (q * k2[r, start : start + BLOCK, :]).astype(jnp.bfloat16)
                s = lax.dot_general(mod, k_win, (((1,), (1,)), ((), ())), preferred_element_type=jnp.float32)
                edge = jnp.where(upper, s[:, :HEAD], s[:, FIRST:])
                score[a % 2, r, :, :HEAD] = edge
                score[a % 2, r, :, HEAD:] = s[:, HEAD:FIRST]
                return jnp.maximum(
                    jnp.maximum(edge, s[:, HEAD : 2 * HEAD]),
                    jnp.maximum(s[:, 2 * HEAD : 3 * HEAD], s[:, 3 * HEAD : FIRST]),
                )

            def mixed(a, r, shift, v_win=v_win):
                start = SECOND - STEP * a
                parts = [
                    jnp.exp2(score[a % 2, r, :, k * HEAD : (k + 1) * HEAD] * SCALE - shift)
                    for k in range(FIRST // HEAD)
                ]
                nothing = jnp.zeros_like(parts[0])
                ends = [jnp.where(upper, parts[0], nothing), jnp.where(upper, nothing, parts[0])]
                weights = jnp.concatenate(ends[:1] + parts[1:] + ends[1:], axis=1).astype(jnp.bfloat16)
                mix = jnp.dot(weights, v_win, preferred_element_type=jnp.float32)
                return mix * v2[r, start : start + BLOCK, :]

            most = None
            for r in range(STEP):
                here = scored(0, r)
                most = here if most is None else jnp.maximum(most, here)
            for a in range(SECOND // STEP):
                new = jnp.max(most, axis=1, keepdims=True)
                if a > 0:
                    old = top[...]
                    new = jnp.maximum(old, new)
                else:
                    new = jnp.broadcast_to(new, (BLOCK, HEAD))
                top[...] = new
                shift = new * SCALE
                if a > 0:
                    shrink = jnp.exp2(old * SCALE - shift)
                    total[...] = total[...] * jnp.concatenate([shrink, shrink], axis=1)
                most = None
                for r in range(STEP):
                    if a + 1 < SECOND // STEP:
                        here = scored(a + 1, r)
                        most = here if most is None else jnp.maximum(most, here)
                    part = mixed(a, r, shift)
                    if a == 0 and r == 0:
                        total[...] = part
                    else:
                        total[...] += part
            out[base : base + BLOCK, g * HEAD : (g + 1) * HEAD] = (
                total[:, :HEAD] / total[:, HEAD:]
            ).astype(jnp.bfloat16)


def attention(index, *operands):
    vmem = pl.BlockSpec(memory_space=pltpu.VMEM)
    hbm = pl.BlockSpec(memory_space=pl.ANY)
    return pl.pallas_call(
        attend,
        out_shape=jax.ShapeDtypeStruct((ROWS, GROUP * HEAD), jnp.bfloat16),
        in_specs=[pl.BlockSpec(memory_space=pltpu.SMEM)] + [hbm] * 7,
        out_specs=vmem,
        scratch_shapes=[pltpu.VMEM(x.shape, x.dtype) for x in operands]
        + [
            pltpu.SemaphoreType.DMA((7,)),
            pltpu.VMEM((3 * ROWS, HEAD), jnp.bfloat16),
            pltpu.VMEM((3 * ROWS, 2 * HEAD), jnp.bfloat16),
            pltpu.VMEM((STEP, BLOCK + SECOND, HEAD), jnp.float32),
            pltpu.VMEM((STEP, BLOCK + SECOND, 2 * HEAD), jnp.float32),
            pltpu.VMEM((3, BLOCK + SECOND, HEAD), jnp.float32),
            pltpu.VMEM((2, STEP, BLOCK, FIRST), jnp.float32),
            pltpu.VMEM((BLOCK, 2 * HEAD), jnp.float32),
            pltpu.VMEM((BLOCK, HEAD), jnp.float32),
        ],
        cost_estimate=pl.CostEstimate(flops=12_000_000_000, bytes_accessed=1_000_000, transcendentals=9_000_000),
        name="attend",
    )(index, *operands)


def project(order, direct, swapped, weight, out, rows, held, total, sems):
    part = weight.shape[0] // CHUNKS
    copies = [
        pltpu.make_async_copy(weight.at[pl.ds(n * part, part)], held.at[pl.ds(n * part, part)], sems.at[n])
        for n in range(CHUNKS)
    ]
    for copy in copies:
        copy.start()
    for k in range(SIDE):
        at = order[k]
        rows[:, k * GROUP * HEAD : (k + 1) * GROUP * HEAD] = jnp.where(
            order[SIDE + k] == 0, direct[at], swapped[at]
        )
    for n in range(CHUNKS):
        copies[n].wait()
        to = slice(n * part, (n + 1) * part)
        piece = jnp.dot(rows[:, to], held[to, :], preferred_element_type=jnp.float32)
        if n == 0:
            total[...] = piece
        elif n < CHUNKS - 1:
            total[...] += piece
        else:
            out[...] = (total[...] + piece).astype(jnp.bfloat16)


def projection(order, direct, swapped, weight):
    depth, width = weight.shape
    vmem = pl.BlockSpec(memory_space=pltpu.VMEM)
    return pl.pallas_call(
        project,
        out_shape=jax.ShapeDtypeStruct((ROWS, width), jnp.bfloat16),
        in_specs=[pl.BlockSpec(memory_space=pltpu.SMEM)] + [vmem] * 2 + [pl.BlockSpec(memory_space=pl.ANY)],
        out_specs=vmem,
        scratch_shapes=[
            pltpu.VMEM((ROWS, depth), jnp.bfloat16),
            pltpu.VMEM((depth, width), jnp.bfloat16),
            pltpu.VMEM((ROWS, width), jnp.float32),
            pltpu.SemaphoreType.DMA((CHUNKS,)),
        ],
        compiler_params=pltpu.CompilerParams(vmem_limit_bytes=62 * 1024 * 1024),
        cost_estimate=pl.CostEstimate(flops=1_100_000_000, bytes_accessed=6_000_000, transcendentals=0),
        name="project",
    )(order, direct, swapped, weight)


CHUNKS = 2
SIDE = 8
CHIPS = 4
HOPS = (0, 1, 3, 2)
Z_GROUPS = [[y * SIDE + z for z in range(SIDE)] for y in range(SIDE)]
Y_GROUPS = [[y * SIDE + z for y in range(SIDE)] for z in range(SIDE)]


def spread(x, groups):
    copies = jnp.broadcast_to(x[None], (SIDE,) + x.shape)
    return lax.all_to_all(copies, "seq", split_axis=0, concat_axis=0, axis_index_groups=groups)


def shifted(x, by):
    size = lax.axis_size("seq")
    return lax.ppermute(x, "seq", [(i, i + by) for i in range(size - by)])


def pack(keys, values, second_keys, second_values, out, sems):
    tail = pl.ds(ROWS - SECOND, SECOND)
    moves = [
        pltpu.make_async_copy(keys, out.at[pl.ds(0, ROWS)], sems.at[0]),
        pltpu.make_async_copy(values, out.at[pl.ds(ROWS, ROWS)], sems.at[1]),
        pltpu.make_async_copy(second_keys.at[tail], out.at[pl.ds(2 * ROWS, SECOND)], sems.at[2]),
        pltpu.make_async_copy(second_values.at[tail], out.at[pl.ds(2 * ROWS + SECOND, SECOND)], sems.at[3]),
    ]
    for move in moves:
        move.start()
    for move in moves:
        move.wait()


def packing(*operands):
    return pl.pallas_call(
        pack,
        out_shape=jax.ShapeDtypeStruct((2 * ROWS + 2 * SECOND, HEAD), jnp.bfloat16),
        in_specs=[pl.BlockSpec(memory_space=pl.ANY)] * 4,
        out_specs=pl.BlockSpec(memory_space=pltpu.VMEM),
        scratch_shapes=[pltpu.SemaphoreType.DMA((4,))],
        cost_estimate=pl.CostEstimate(flops=0, bytes_accessed=300_000, transcendentals=0),
        name="pack",
    )(*operands)


def relay(block, out, sem):
    move = pltpu.make_async_copy(block, out, sem)
    move.start()
    move.wait()


def relayed(block):
    return pl.pallas_call(
        relay,
        out_shape=jax.ShapeDtypeStruct(block.shape, block.dtype),
        in_specs=[pl.BlockSpec(memory_space=pltpu.VMEM)],
        out_specs=pl.BlockSpec(memory_space=pl.ANY),
        scratch_shapes=[pltpu.SemaphoreType.DMA],
        compiler_params=pltpu.CompilerParams(vmem_limit_bytes=16 * 1024 * 1024),
        cost_estimate=pl.CostEstimate(flops=0, bytes_accessed=1_000_000, transcendentals=0),
        name="relay",
    )(block)


def on_device(queries, first_keys, first_values, second_keys, second_values, out_weight):
    width = out_weight.shape[1]
    packed = packing(first_keys, first_values, second_keys, second_values)
    near = shifted(packed, 1)
    far = shifted(packed, 2)
    block = spread(out_weight, Z_GROUPS)
    block = relayed(block)
    weight = lax.all_gather(
        block.reshape(ROWS, width), "seq", axis=0, tiled=True, axis_index_groups=Y_GROUPS
    )
    seq = lax.axis_index("seq").astype(jnp.int32)
    head = lax.axis_index("head").astype(jnp.int32)
    attended = attention(
        seq.reshape(1), queries, far, near, first_keys, first_values, second_keys, second_values
    )
    direct = [attended]
    for hop in HOPS[1:]:
        pairs = [(2 * x + c, 2 * ((x + hop) % CHIPS) + c) for x in range(CHIPS) for c in range(2)]
        direct.append(lax.ppermute(attended, "head", pairs))
    direct = jnp.stack(direct)
    swapped = lax.ppermute(direct, "head", [(2 * x + c, 2 * x + 1 - c) for x in range(CHIPS) for c in range(2)])
    chip, core = lax.div(head, 2), lax.rem(head, 2)
    owner = jnp.arange(SIDE, dtype=jnp.int32)
    distance = lax.rem(chip - lax.div(owner, 2) + CHIPS, CHIPS)
    place = jnp.where(distance < 2, distance, 5 - distance)
    part = jnp.where(lax.rem(owner, 2) == core, 0, 1)
    order = jnp.concatenate([place, part]).astype(jnp.int32)
    return attended, projection(order, direct, swapped, weight)


def solution(mesh):
    spec = P("seq", "head")

    return jax.shard_map(on_device, mesh=mesh, in_specs=(spec,) * 6, out_specs=(spec, spec), check_vma=False)
```

```python
import math

import jax
import jax.numpy as jnp
from jax import lax
from jax.experimental import pallas as pl
from jax.experimental.pallas import tpu as pltpu
from jax.sharding import PartitionSpec as P


HEAD = 128
GROUP = 2
FIRST = 512
SECOND = 32
ROWS = 256
BLOCK = 128
KEYS = FIRST + BLOCK
STEP = 8
SCALE = HEAD ** (-0.5) * math.log2(math.e)


def attend(index, *refs):
    sources, out, held_refs, sems = refs[:7], refs[7], refs[8:15], refs[15]
    k_all, v_all, k2, v2, kept, score, total, top = refs[16:]
    moves = [pltpu.make_async_copy(src, dst, sems.at[i]) for i, (src, dst) in enumerate(zip(sources, held_refs))]
    for move in moves:
        move.start()
    for move in moves:
        move.wait()
    queries, far, near, keys, values, second_keys, second_values = held_refs
    first_block = index[0]
    spare = jnp.broadcast_to(keys[0:1, :].astype(jnp.float32), (ROWS, HEAD)).astype(jnp.bfloat16)
    zero = jnp.zeros((ROWS, HEAD), jnp.bfloat16)
    one = jnp.ones((ROWS, HEAD), jnp.bfloat16)
    row = lax.broadcasted_iota(jnp.int32, (BLOCK, HEAD), 0)
    col = lax.broadcasted_iota(jnp.int32, (BLOCK, HEAD), 1)
    upper = col > row

    for slot, source in enumerate((far, near)):
        held = first_block >= 2 - slot
        to = slice(slot * ROWS, (slot + 1) * ROWS)
        k_all[to, :] = jnp.where(held, source[:ROWS, :], spare)
        v_all[to, :HEAD] = jnp.where(held, source[ROWS : 2 * ROWS, :], zero)
        v_all[to, HEAD:] = jnp.where(held, one, zero)
    k_all[2 * ROWS :, :] = keys[...]
    v_all[2 * ROWS :, :HEAD] = values[...]
    v_all[2 * ROWS :, HEAD:] = one

    for b in range(ROWS // BLOCK):
        base = b * BLOCK
        if b == 0:
            held = first_block >= 1
            edge_k = near[2 * ROWS : 2 * ROWS + SECOND, :].astype(jnp.float32)
            edge_v = near[2 * ROWS + SECOND : 2 * ROWS + 2 * SECOND, :].astype(jnp.float32)
            spare2 = jnp.broadcast_to(second_keys[0:1, :].astype(jnp.float32), (SECOND, HEAD))
            kept[0, 0:SECOND, :] = jnp.where(held, edge_k, spare2)
            kept[1, 0:SECOND, :] = jnp.where(held, edge_v, jnp.zeros_like(edge_v))
            kept[2, 0:SECOND, :] = jnp.where(held, jnp.ones_like(edge_v), jnp.zeros_like(edge_v))
            kept[0, SECOND:, :] = second_keys[:BLOCK, :].astype(jnp.float32)
            kept[1, SECOND:, :] = second_values[:BLOCK, :].astype(jnp.float32)
            kept[2, SECOND:, :] = jnp.ones((BLOCK, HEAD), jnp.float32)
        else:
            kept[0] = second_keys[base - SECOND : base + BLOCK, :].astype(jnp.float32)
            kept[1] = second_values[base - SECOND : base + BLOCK, :].astype(jnp.float32)
        for r in range(STEP):
            k2[r, STEP:, :] = kept[0, STEP - r : SECOND + BLOCK - r, :]
            v2[r, STEP:, :HEAD] = kept[1, STEP - r : SECOND + BLOCK - r, :]
            if b == 0:
                v2[r, STEP:, HEAD:] = kept[2, STEP - r : SECOND + BLOCK - r, :]
            else:
                v2[r, STEP:, HEAD:] = jnp.ones((SECOND + BLOCK - STEP, HEAD), jnp.float32)

        k_win = k_all[base : base + KEYS, :]
        v_win = v_all[base : base + KEYS, :]
        for g in range(GROUP):
            q = queries[base : base + BLOCK, g * HEAD : (g + 1) * HEAD].astype(jnp.float32)

            def scored(a, r, q=q, k_win=k_win):
                start = SECOND - STEP * a
                mod = (q * k2[r, start : start + BLOCK, :]).astype(jnp.bfloat16)
                s = lax.dot_general(mod, k_win, (((1,), (1,)), ((), ())), preferred_element_type=jnp.float32)
                edge = jnp.where(upper, s[:, :HEAD], s[:, FIRST:])
                score[a % 2, r, :, :HEAD] = edge
                score[a % 2, r, :, HEAD:] = s[:, HEAD:FIRST]
                return jnp.maximum(
                    jnp.maximum(edge, s[:, HEAD : 2 * HEAD]),
                    jnp.maximum(s[:, 2 * HEAD : 3 * HEAD], s[:, 3 * HEAD : FIRST]),
                )

            def mixed(a, r, shift, v_win=v_win):
                start = SECOND - STEP * a
                parts = [
                    jnp.exp2(score[a % 2, r, :, k * HEAD : (k + 1) * HEAD] * SCALE - shift)
                    for k in range(FIRST // HEAD)
                ]
                nothing = jnp.zeros_like(parts[0])
                ends = [jnp.where(upper, parts[0], nothing), jnp.where(upper, nothing, parts[0])]
                weights = jnp.concatenate(ends[:1] + parts[1:] + ends[1:], axis=1).astype(jnp.bfloat16)
                mix = jnp.dot(weights, v_win, preferred_element_type=jnp.float32)
                return mix * v2[r, start : start + BLOCK, :]

            most = None
            for r in range(STEP):
                here = scored(0, r)
                most = here if most is None else jnp.maximum(most, here)
            for a in range(SECOND // STEP):
                new = jnp.max(most, axis=1, keepdims=True)
                if a > 0:
                    old = top[...]
                    new = jnp.maximum(old, new)
                else:
                    new = jnp.broadcast_to(new, (BLOCK, HEAD))
                top[...] = new
                shift = new * SCALE
                if a > 0:
                    shrink = jnp.exp2(old * SCALE - shift)
                    total[...] = total[...] * jnp.concatenate([shrink, shrink], axis=1)
                most = None
                for r in range(STEP):
                    if a + 1 < SECOND // STEP:
                        here = scored(a + 1, r)
                        most = here if most is None else jnp.maximum(most, here)
                    part = mixed(a, r, shift)
                    if a == 0 and r == 0:
                        total[...] = part
                    else:
                        total[...] += part
            out[base : base + BLOCK, g * HEAD : (g + 1) * HEAD] = (
                total[:, :HEAD] / total[:, HEAD:]
            ).astype(jnp.bfloat16)


def attention(index, *operands):
    vmem = pl.BlockSpec(memory_space=pltpu.VMEM)
    hbm = pl.BlockSpec(memory_space=pl.ANY)
    return pl.pallas_call(
        attend,
        out_shape=jax.ShapeDtypeStruct((ROWS, GROUP * HEAD), jnp.bfloat16),
        in_specs=[pl.BlockSpec(memory_space=pltpu.SMEM)] + [hbm] * 7,
        out_specs=vmem,
        scratch_shapes=[pltpu.VMEM(x.shape, x.dtype) for x in operands]
        + [
            pltpu.SemaphoreType.DMA((7,)),
            pltpu.VMEM((3 * ROWS, HEAD), jnp.bfloat16),
            pltpu.VMEM((3 * ROWS, 2 * HEAD), jnp.bfloat16),
            pltpu.VMEM((STEP, BLOCK + SECOND, HEAD), jnp.float32),
            pltpu.VMEM((STEP, BLOCK + SECOND, 2 * HEAD), jnp.float32),
            pltpu.VMEM((3, BLOCK + SECOND, HEAD), jnp.float32),
            pltpu.VMEM((2, STEP, BLOCK, FIRST), jnp.float32),
            pltpu.VMEM((BLOCK, 2 * HEAD), jnp.float32),
            pltpu.VMEM((BLOCK, HEAD), jnp.float32),
        ],
        cost_estimate=pl.CostEstimate(flops=12_000_000_000, bytes_accessed=1_000_000, transcendentals=9_000_000),
        name="attend",
    )(index, *operands)


def project(order, direct, swapped, weight, out, rows, held, total, sems):
    part = weight.shape[0] // CHUNKS
    copies = [
        pltpu.make_async_copy(weight.at[pl.ds(n * part, part)], held.at[pl.ds(n * part, part)], sems.at[n])
        for n in range(CHUNKS)
    ]
    for copy in copies:
        copy.start()
    for k in range(SIDE):
        at = order[k]
        rows[:, k * GROUP * HEAD : (k + 1) * GROUP * HEAD] = jnp.where(
            order[SIDE + k] == 0, direct[at], swapped[at]
        )
    for n in range(CHUNKS):
        copies[n].wait()
        to = slice(n * part, (n + 1) * part)
        piece = jnp.dot(rows[:, to], held[to, :], preferred_element_type=jnp.float32)
        if n == 0:
            total[...] = piece
        elif n < CHUNKS - 1:
            total[...] += piece
        else:
            out[...] = (total[...] + piece).astype(jnp.bfloat16)


def projection(order, direct, swapped, weight):
    depth, width = weight.shape
    vmem = pl.BlockSpec(memory_space=pltpu.VMEM)
    return pl.pallas_call(
        project,
        out_shape=jax.ShapeDtypeStruct((ROWS, width), jnp.bfloat16),
        in_specs=[pl.BlockSpec(memory_space=pltpu.SMEM)] + [vmem] * 2 + [pl.BlockSpec(memory_space=pl.ANY)],
        out_specs=vmem,
        scratch_shapes=[
            pltpu.VMEM((ROWS, depth), jnp.bfloat16),
            pltpu.VMEM((depth, width), jnp.bfloat16),
            pltpu.VMEM((ROWS, width), jnp.float32),
            pltpu.SemaphoreType.DMA((CHUNKS,)),
        ],
        compiler_params=pltpu.CompilerParams(vmem_limit_bytes=62 * 1024 * 1024),
        cost_estimate=pl.CostEstimate(flops=1_100_000_000, bytes_accessed=6_000_000, transcendentals=0),
        name="project",
    )(order, direct, swapped, weight)


CHUNKS = 2
SIDE = 8
CHIPS = 4
HOPS = (0, 1, 3, 2)
Z_GROUPS = [[y * SIDE + z for z in range(SIDE)] for y in range(SIDE)]
Y_GROUPS = [[y * SIDE + z for y in range(SIDE)] for z in range(SIDE)]


def repeat(x, out):
    for k in range(SIDE):
        out[k] = x[...]


def spread(x, groups):
    vmem = pl.BlockSpec(memory_space=pltpu.VMEM)
    copies = pl.pallas_call(
        repeat,
        out_shape=jax.ShapeDtypeStruct((SIDE,) + x.shape, x.dtype),
        in_specs=[vmem],
        out_specs=vmem,
        compiler_params=pltpu.CompilerParams(vmem_limit_bytes=16 * 1024 * 1024),
        cost_estimate=pl.CostEstimate(flops=0, bytes_accessed=600_000, transcendentals=0),
        name="repeat",
    )(x)
    return lax.all_to_all(copies, "seq", split_axis=0, concat_axis=0, axis_index_groups=groups)


def shifted(x, by):
    size = lax.axis_size("seq")
    return lax.ppermute(x, "seq", [(i, i + by) for i in range(size - by)])


def pack(keys, values, second_keys, second_values, out, sems):
    tail = pl.ds(ROWS - SECOND, SECOND)
    moves = [
        pltpu.make_async_copy(keys, out.at[pl.ds(0, ROWS)], sems.at[0]),
        pltpu.make_async_copy(values, out.at[pl.ds(ROWS, ROWS)], sems.at[1]),
        pltpu.make_async_copy(second_keys.at[tail], out.at[pl.ds(2 * ROWS, SECOND)], sems.at[2]),
        pltpu.make_async_copy(second_values.at[tail], out.at[pl.ds(2 * ROWS + SECOND, SECOND)], sems.at[3]),
    ]
    for move in moves:
        move.start()
    for move in moves:
        move.wait()


def packing(*operands):
    return pl.pallas_call(
        pack,
        out_shape=jax.ShapeDtypeStruct((2 * ROWS + 2 * SECOND, HEAD), jnp.bfloat16),
        in_specs=[pl.BlockSpec(memory_space=pl.ANY)] * 4,
        out_specs=pl.BlockSpec(memory_space=pltpu.VMEM),
        scratch_shapes=[pltpu.SemaphoreType.DMA((4,))],
        cost_estimate=pl.CostEstimate(flops=0, bytes_accessed=300_000, transcendentals=0),
        name="pack",
    )(*operands)


def relay(block, out, sem):
    move = pltpu.make_async_copy(block, out, sem)
    move.start()
    move.wait()


def relayed(block):
    return pl.pallas_call(
        relay,
        out_shape=jax.ShapeDtypeStruct(block.shape, block.dtype),
        in_specs=[pl.BlockSpec(memory_space=pltpu.VMEM)],
        out_specs=pl.BlockSpec(memory_space=pl.ANY),
        scratch_shapes=[pltpu.SemaphoreType.DMA],
        compiler_params=pltpu.CompilerParams(vmem_limit_bytes=16 * 1024 * 1024),
        cost_estimate=pl.CostEstimate(flops=0, bytes_accessed=1_000_000, transcendentals=0),
        name="relay",
    )(block)


def on_device(queries, first_keys, first_values, second_keys, second_values, out_weight):
    width = out_weight.shape[1]
    packed = packing(first_keys, first_values, second_keys, second_values)
    near = shifted(packed, 1)
    far = shifted(packed, 2)
    block = spread(out_weight, Z_GROUPS)
    block = relayed(block)
    weight = lax.all_gather(
        block.reshape(ROWS, width), "seq", axis=0, tiled=True, axis_index_groups=Y_GROUPS
    )
    seq = lax.axis_index("seq").astype(jnp.int32)
    head = lax.axis_index("head").astype(jnp.int32)
    attended = attention(
        seq.reshape(1), queries, far, near, first_keys, first_values, second_keys, second_values
    )
    direct = [attended]
    for hop in HOPS[1:]:
        pairs = [(2 * x + c, 2 * ((x + hop) % CHIPS) + c) for x in range(CHIPS) for c in range(2)]
        direct.append(lax.ppermute(attended, "head", pairs))
    direct = jnp.stack(direct)
    swapped = lax.ppermute(direct, "head", [(2 * x + c, 2 * x + 1 - c) for x in range(CHIPS) for c in range(2)])
    chip, core = lax.div(head, 2), lax.rem(head, 2)
    owner = jnp.arange(SIDE, dtype=jnp.int32)
    distance = lax.rem(chip - lax.div(owner, 2) + CHIPS, CHIPS)
    place = jnp.where(distance < 2, distance, 5 - distance)
    part = jnp.where(lax.rem(owner, 2) == core, 0, 1)
    order = jnp.concatenate([place, part]).astype(jnp.int32)
    return attended, projection(order, direct, swapped, weight)


def solution(mesh):
    spec = P("seq", "head")

    return jax.shard_map(on_device, mesh=mesh, in_specs=(spec,) * 6, out_specs=(spec, spec), check_vma=False)
```
